32 devices in a mesh: ctx: 8 (over y, x, core), head: 4 (over z).
Axes of the slice: x: 2, y: 2, z: 4, core: 2. Of those that a mesh axis runs over, the one named last changes fastest.
Arguments:
- prompt_values: bfloat16 [4096, 8192], P('ctx', 'head'), may hold values from -6 to 6
- prompt_gate: bfloat16 [4096, 8192], P('ctx', 'head'), may hold values from -6 to 6
- prompt_inject: bfloat16 [4096, 4, 256], P('ctx', 'head'), may hold values from -6 to 6
- prompt_read: bfloat16 [4096, 4, 256], P('ctx', 'head'), may hold values from -0.375 to 0.375
- prompt_step: float32 [128, 4096], P('head', 'ctx'), may hold values from -8 to 256
- decay_log: float32 [128], P('head'), may hold values from -10 to 0
- skip_gain: float32 [128], P('head'), may hold values from 0.5 to 1.5
- norm_weight: float32 [8192], P('head'), may hold values from 0.1 to 1.9
- out_weight: bfloat16 [8192, 4096], P('head'), may hold values from -0.0625 to 0.0625
- sample_values: bfloat16 [16, 16, 8192], P('ctx', None, 'head'), may hold values from -6 to 6
- sample_gate: bfloat16 [16, 16, 8192], P('ctx', None, 'head'), may hold values from -6 to 6
- sample_inject: bfloat16 [16, 16, 4, 256], P('ctx', None, 'head'), may hold values from -6 to 6
- sample_read: bfloat16 [16, 16, 4, 256], P('ctx', None, 'head'), may hold values from -0.375 to 0.375
- sample_step: float32 [128, 16, 16], P('head', 'ctx'), may hold values from -8 to 256
- sample_length: int32 [16], P('ctx'), may hold values from 1 to 16
Outputs:
- prompt_mixed: bfloat16 [4096, 4096], P('head', 'ctx')
- sample_mixed: bfloat16 [4096, 16], P('head', 'ctx')
The draws below stay inside these ranges and needn't reach their ends.
All inputs are finite; a program needn't handle non-finite values.
Results may differ from the reference program's by a relative error of at most 0.02.
Values may be sent and summed in bfloat16 or wider, within the bound.
A program may use at most 192 MiB of HBM per device.

```python
import jax
import jax.numpy as jnp
from jax import lax

LOCAL_HEAD_COUNT = 128
HEAD_DIM = 64
STATE = 256
HEAD_GROUPS = 4
OUT_COLS = 4096
BLOCK = 128
SLEN = 16
TOK_DEV = 512
NTOK = 4096
SAMPLES = 16


def head_memory(key):
    base_key = jax.random.fold_in(key, 11)
    sorter, spreader = jax.random.split(base_key, 2)
    chooser = jax.random.uniform(sorter, (LOCAL_HEAD_COUNT,), jnp.float32)
    fast_share = 0.3
    middle_share = 0.5
    position = jax.random.uniform(spreader, (LOCAL_HEAD_COUNT,), jnp.float32)
    fast_memory = 30.0 * (5.0 / 3.0) ** position
    middle_memory = 50.0 * (2.5 * NTOK / 50.0) ** position
    slow_memory = 2.5 * NTOK * 2.4 ** position
    return jnp.where(chooser < fast_share, fast_memory, jnp.where(chooser < middle_share, middle_memory, slow_memory))


def spike_mask(key):
    places = jax.random.randint(jax.random.fold_in(key, 23), (HEAD_GROUPS, 2), 0, NTOK)
    positions = jnp.arange(NTOK)
    return jnp.any(positions[:, None, None] == places[None], axis=2)


def draw_decay_log(key, part):
    return (-0.5 * jnp.log(head_memory(key))).astype(jnp.float32)


def draw_prompt_step(key, part):
    memory = head_memory(key)
    decay_velocity = memory ** (-0.5)
    token_key, device_key, keeper_key = jax.random.split(jax.random.fold_in(key, 37), 3)
    token_factor = jnp.exp(jax.random.uniform(token_key, (LOCAL_HEAD_COUNT, NTOK), jnp.float32, -0.7, 0.7))
    device_factor = jnp.exp(jax.random.uniform(device_key, (LOCAL_HEAD_COUNT, NTOK // TOK_DEV), jnp.float32, -0.7, 0.7))
    stable_state = decay_velocity[:, None] * token_factor * jnp.repeat(device_factor, TOK_DEV, axis=1)
    retained_fraction = jax.random.uniform(keeper_key, (LOCAL_HEAD_COUNT, NTOK), jnp.float32, 0.5, 0.8)
    spike_steps = jnp.minimum(-jnp.log(retained_fraction) / decay_velocity[:, None], 250.0)
    inside_spike = jnp.repeat(spike_mask(key).T, LOCAL_HEAD_COUNT // HEAD_GROUPS, axis=0)
    selected_rows = jnp.where(inside_spike, spike_steps, stable_state)
    return (selected_rows + jnp.log(-jnp.expm1(-selected_rows))).astype(jnp.float32)


def draw_sample_step(key, part):
    memory = head_memory(key)
    token_factor = jnp.exp(jax.random.uniform(jax.random.fold_in(key, 53), (LOCAL_HEAD_COUNT, SAMPLES, SLEN), jnp.float32, -0.7, 0.7))
    stable_state = (memory ** (-0.5))[:, None, None] * token_factor
    return (stable_state + jnp.log(-jnp.expm1(-stable_state))).astype(jnp.float32)


def draw_prompt_inject(key, part):
    noise_key = jax.random.fold_in(key, 41)
    raw_noise = jnp.clip(jax.random.normal(noise_key, (NTOK, HEAD_GROUPS, STATE), jnp.float32), -6.0, 6.0)
    attenuation = jnp.where(spike_mask(key)[:, :, None], 0.02, 1.0)
    return (raw_noise * attenuation).astype(jnp.bfloat16)


def touch_ends(array, stream_key, smallest, high):
    spot = [jax.random.randint(jax.random.fold_in(stream_key, axis), (), 0, length) for axis, length in enumerate(array.shape)]
    main_axis = array.shape.index(max(array.shape))
    next_to = spot[:main_axis] + [(spot[main_axis] + 1) % array.shape[main_axis]] + spot[main_axis + 1:]
    return array.at[tuple(spot)].set(smallest).at[tuple(next_to)].set(high)


def steps_of(stream_key, extent, pieces, low, high):
    factor_of, own = 1.0, jax.random.fold_in(stream_key, 6)
    for dim, parts in pieces:
        steps = jnp.exp(jax.random.uniform(jax.random.fold_in(own, dim), (parts,), jnp.float32, low / len(pieces), high / len(pieces)))
        factor_of = factor_of * jnp.repeat(steps, extent[dim] // parts).reshape([-1 if axis == dim else 1 for axis in range(len(extent))])
    return factor_of


def gaussian(stream_key, shape, deviation, reach, pieces=(), dtype=jnp.bfloat16):
    gain = steps_of(stream_key, shape, pieces, -0.22, 0.18) if pieces else 1.0
    array = jax.random.normal(stream_key, shape, jnp.float32) * deviation * gain
    return jnp.minimum(jnp.maximum(array, -reach), reach).astype(dtype)


def setup_inputs(seed: int = 0) -> dict:
    splits = jax.random.split(jax.random.key(seed), 16)
    return {
        "prompt_values": gaussian(splits[0], (NTOK, LOCAL_HEAD_COUNT * HEAD_DIM), 1.0, 6.0, ((0, 8), (1, 4))),
        "prompt_gate": gaussian(splits[1], (NTOK, LOCAL_HEAD_COUNT * HEAD_DIM), 1.0, 6.0, ((0, 8), (1, 4))),
        "prompt_inject": draw_prompt_inject(jax.random.fold_in(splits[15], 71), 0),
        "prompt_read": gaussian(splits[3], (NTOK, HEAD_GROUPS, STATE), STATE ** -0.5, 0.375, ((0, 8), (1, 4))),
        "prompt_step": draw_prompt_step(jax.random.fold_in(splits[15], 71), 0),
        "decay_log": draw_decay_log(jax.random.fold_in(splits[15], 71), 0),
        "skip_gain": jnp.clip(0.5 + 1.0 * jax.random.uniform(splits[6], (LOCAL_HEAD_COUNT,), jnp.float32) ** steps_of(splits[6], (LOCAL_HEAD_COUNT,), ((0, 4),), -0.2, 0.2), 0.5, 1.5),
        "norm_weight": jnp.clip(1.0 + 0.18 * jax.random.normal(splits[7], (LOCAL_HEAD_COUNT * HEAD_DIM,), jnp.float32), 0.1, 1.9),
        "out_weight": gaussian(splits[8], (LOCAL_HEAD_COUNT * HEAD_DIM, OUT_COLS), (LOCAL_HEAD_COUNT * HEAD_DIM) ** -0.5, 0.0625, ((0, 4),)),
        "sample_values": gaussian(splits[9], (SAMPLES, SLEN, LOCAL_HEAD_COUNT * HEAD_DIM), 1.0, 6.0, ((0, 8), (2, 4))),
        "sample_gate": gaussian(splits[10], (SAMPLES, SLEN, LOCAL_HEAD_COUNT * HEAD_DIM), 1.0, 6.0, ((0, 8), (2, 4))),
        "sample_inject": gaussian(splits[11], (SAMPLES, SLEN, HEAD_GROUPS, STATE), 1.0, 6.0, ((0, 8), (2, 4))),
        "sample_read": gaussian(splits[12], (SAMPLES, SLEN, HEAD_GROUPS, STATE), STATE ** -0.5, 0.375, ((0, 8), (2, 4))),
        "sample_step": draw_sample_step(jax.random.fold_in(splits[15], 71), 0),
        "sample_length": touch_ends(jax.random.randint(splits[14], (SAMPLES,), 1, SLEN + 1), jax.random.fold_in(splits[14], 1), 1, SLEN).astype(jnp.int32),
    }


full_precision = lax.Precision.HIGHEST

def block_terms(values, inject, readout, steps, decay_rate):
    length = values.shape[0]
    log_decay = steps * decay_rate[:, None]
    running = jnp.cumsum(log_decay, axis=1)
    scores = jnp.dot(readout.astype(jnp.float32), inject.astype(jnp.float32).T, precision=full_precision)
    causal = jnp.arange(length)[:, None] >= jnp.arange(length)[None, :]
    gap_logs = jnp.where(causal[None], running[:, :, None] - running[:, None, :], 0.0)
    mixing = jnp.where(causal[None], scores[None] * jnp.exp(gap_logs) * steps[:, None, :], 0.0).astype(jnp.bfloat16)
    local_out = jnp.einsum('hts,shp->thp', mixing.astype(jnp.float32), values.astype(jnp.float32), precision=full_precision)
    to_end = jnp.exp(running[:, -1:] - running) * steps
    weighted = (to_end[:, :, None] * inject.astype(jnp.float32)[None]).astype(jnp.bfloat16)
    local_state = jnp.einsum('shp,hsn->hpn', values.astype(jnp.float32), weighted.astype(jnp.float32), precision=full_precision)
    return (local_out, local_state, running)

def group_block(values, inject, readout, steps, decay_rate, carry_state):
    local_out, local_state, running = block_terms(values, inject, readout, steps, decay_rate)
    carried = jnp.einsum('tn,hpn->thp', readout.astype(jnp.float32), carry_state, precision=full_precision)
    carried = carried * jnp.exp(running).T[:, :, None]
    next_state = jnp.exp(running[:, -1])[:, None, None] * carry_state + local_state
    return (local_out + carried, next_state, running)

def finish(outputs, values, gate, skip_gain, norm_weight, groups):
    row_count = values.shape[0]
    with_skip = outputs + skip_gain[None, :, None] * values.reshape(row_count, skip_gain.shape[0], -1).astype(jnp.float32)
    gated_out = with_skip.reshape(row_count, -1) * jax.nn.silu(gate.astype(jnp.float32))
    grouped = gated_out.reshape(row_count, groups, -1)
    inverse_rms = lax.rsqrt(lax.optimization_barrier(jnp.mean(grouped * grouped, axis=2, keepdims=True)) + 1e-05)
    return ((grouped * inverse_rms).reshape(row_count, -1) * norm_weight[None]).astype(jnp.bfloat16)

def reference(prompt_values, prompt_gate, prompt_inject, prompt_read, prompt_step, decay_log, skip_gain, norm_weight, out_weight, sample_values, sample_gate, sample_inject, sample_read, sample_step, sample_length):
    per_group = LOCAL_HEAD_COUNT // HEAD_GROUPS
    blocks = NTOK // BLOCK
    decay_rate = (-jnp.exp(decay_log)).reshape(HEAD_GROUPS, per_group)
    steps = jax.nn.softplus(prompt_step).reshape(HEAD_GROUPS, per_group, blocks, BLOCK).transpose(2, 0, 1, 3)
    values = prompt_values.reshape(blocks, BLOCK, HEAD_GROUPS, per_group, HEAD_DIM)
    inject = prompt_inject.reshape(blocks, BLOCK, HEAD_GROUPS, STATE)
    readout = prompt_read.reshape(blocks, BLOCK, HEAD_GROUPS, STATE)
    grouped_block = jax.vmap(group_block, in_axes=(1, 1, 1, 0, 0, 0), out_axes=(1, 0, 0))

    def advance(carry_state, block_data):
        block_values, block_inject, block_readout, block_steps = block_data
        block_out, next_state, running = grouped_block(block_values, block_inject, block_readout, block_steps, decay_rate, carry_state)
        return (next_state, block_out)
    start_state = jnp.zeros((HEAD_GROUPS, per_group, HEAD_DIM, STATE), jnp.float32)
    final_state, outputs = lax.scan(advance, start_state, (values, inject, readout, steps))
    outputs = outputs.reshape(NTOK, LOCAL_HEAD_COUNT, HEAD_DIM)
    normed = finish(outputs, prompt_values, prompt_gate, skip_gain, norm_weight, HEAD_GROUPS)
    weight_full = out_weight.astype(jnp.float32)
    prompt_mixed = jnp.dot(normed.astype(jnp.float32), weight_full, precision=full_precision).T.astype(jnp.bfloat16)
    sample_steps = jax.nn.softplus(sample_step).reshape(HEAD_GROUPS, per_group, SAMPLES, SLEN).transpose(2, 0, 1, 3)
    sample_vals = sample_values.reshape(SAMPLES, SLEN, HEAD_GROUPS, per_group, HEAD_DIM)
    per_sample = jax.vmap(grouped_block, in_axes=(0, 0, 0, 0, None, None), out_axes=(0, 0, 0))
    sample_out = per_sample(sample_vals, sample_inject, sample_read, sample_steps, decay_rate, final_state)[0]
    sample_out = sample_out.reshape(SAMPLES * SLEN, LOCAL_HEAD_COUNT, HEAD_DIM)
    sample_normed = finish(sample_out, sample_values.reshape(SAMPLES * SLEN, -1), sample_gate.reshape(SAMPLES * SLEN, -1), skip_gain, norm_weight, HEAD_GROUPS)
    onehot = (jnp.arange(SLEN)[None, :] == (sample_length - 1)[:, None]).astype(jnp.float32)
    picked = lax.optimization_barrier(jnp.sum(onehot[:, :, None] * sample_normed.reshape(SAMPLES, SLEN, -1).astype(jnp.float32), axis=1)).astype(jnp.bfloat16)
    sample_mixed = jnp.dot(picked.astype(jnp.float32), weight_full, precision=full_precision).T.astype(jnp.bfloat16)
    return (prompt_mixed, sample_mixed)
```

```python
import functools

import jax
import jax.numpy as jnp
from jax import lax
from jax.experimental import pallas as pl
from jax.experimental.pallas import tpu as pltpu
from jax.sharding import PartitionSpec as P

BLOCK = 128
LANES = 128
PAD = 8
F32 = jnp.float32
BF16 = jnp.bfloat16
EXACT = lax.Precision.HIGHEST
VMEM_LIMIT = 60 * 1024 * 1024


def dot(a, b, dims=((1,), (0,)), precision=None):
    return lax.dot_general(a, b, (dims, ((), ())), precision=precision, preferred_element_type=F32)


def softplus(v):
    return jnp.maximum(v, 0.0) + jnp.log1p(jnp.exp(-jnp.abs(v)))


def silu(v):
    return v / (1.0 + jnp.exp(-v))


def spread(w, expander):
    high = w.astype(BF16)
    low = (w - high.astype(F32)).astype(BF16)
    return dot(jnp.concatenate([high, low], axis=1), expander)


def expander_of(heads, dim):
    row = lax.broadcasted_iota(jnp.int32, (2 * heads, heads * dim), 0)
    lane = lax.broadcasted_iota(jnp.int32, (2 * heads, heads * dim), 1)
    head = lane // dim
    return jnp.where((row == head) | (row == head + heads), 1.0, 0.0).astype(BF16)


def square(n):
    return (
        lax.broadcasted_iota(jnp.int32, (n, n), 0),
        lax.broadcasted_iota(jnp.int32, (n, n), 1),
    )


def state_kernel(dim, values_ref, inject_ref, step_ref, rate_ref, state_ref, log_ref, scaled_ref):
    tokens, channels = values_ref.shape
    heads = channels // dim
    steps = softplus(step_ref[...])
    logs = steps * rate_ref[...]
    i, j = square(tokens)
    after = dot(jnp.where(j > i, 1.0, 0.0), logs, ((1,), (1,)), EXACT)
    total = dot(jnp.ones((PAD, tokens), F32), logs, ((1,), (1,)), EXACT)
    turned = dot(jnp.where(i == j, 1.0, 0.0), steps, ((1,), (1,)), EXACT)
    weight = jnp.exp(after) * turned
    expander = expander_of(heads, dim)
    for b in range(tokens // BLOCK):
        rows = pl.ds(b * BLOCK, BLOCK)
        wide = spread(weight[b * BLOCK : (b + 1) * BLOCK], expander)
        scaled_ref[rows, :] = (wide * values_ref[rows, :].astype(F32)).astype(BF16)
    state_ref[...] = dot(inject_ref[...], scaled_ref[...], ((0,), (0,))).astype(BF16)
    log_ref[...] = dot(total, expander[:heads].astype(F32), precision=EXACT)


def local_kernel(
    dim,
    values_ref,
    gate_ref,
    inject_ref,
    read_ref,
    step_ref,
    rate_ref,
    skip_ref,
    out_ref,
    gain_ref,
    state_ref,
    offset_ref,
    part_ref,
):
    channels = values_ref.shape[1]
    heads = channels // dim

    @pl.when(pl.program_id(0) == 0)
    def _():
        state_ref[...] = jnp.zeros_like(state_ref)
        offset_ref[...] = jnp.zeros_like(offset_ref)

    steps = softplus(step_ref[...])
    logs = steps * rate_ref[...]
    i, j = square(BLOCK)
    lower = jnp.where(i >= j, 1.0, 0.0)
    running = dot(logs, lower, ((1,), (1,)), EXACT)
    running_t = dot(lower, logs, ((1,), (1,)), EXACT)
    after = dot(jnp.where(j > i, 1.0, 0.0), logs, ((1,), (1,)), EXACT)
    turned = dot(jnp.where(i == j, 1.0, 0.0), steps, ((1,), (1,)), EXACT)
    expander = expander_of(heads, dim)
    inject = inject_ref[...]
    readout = read_ref[...]
    scores = jnp.where(i >= j, dot(readout, inject, ((1,), (1,))), 0.0)
    per = LANES // dim
    lane = lax.broadcasted_iota(jnp.int32, (BLOCK, LANES), 1)
    for k in range(heads // per):
        cols = slice(k * LANES, (k + 1) * LANES)
        pair = values_ref[:, cols]
        mixes, parts = [], []
        for q in range(per):
            h = k * per + q
            gap = jnp.minimum(running_t[:, h : h + 1] - running[h : h + 1, :], 0.0)
            mixes.append((scores * jnp.exp(gap) * steps[h : h + 1, :]).astype(BF16))
            parts.append(jnp.where(lane // dim == q, pair, jnp.zeros_like(pair)))
        part_ref[:, cols] = dot(jnp.concatenate(mixes, axis=1), jnp.concatenate(parts, axis=0))
    decay = spread(jnp.exp(running_t), expander)
    values = values_ref[...].astype(F32)
    opened = silu(gate_ref[...].astype(F32))
    total = part_ref[...] + skip_ref[...] * values
    total = total + dot(readout, state_ref[...].astype(BF16)) * decay
    out_ref[...] = (total * opened).astype(BF16)
    offset = offset_ref[0:1, :]
    gain_ref[...] = (opened * spread(jnp.exp(running_t + offset), expander)).astype(BF16)
    offset_ref[0:1, :] = offset + running_t[BLOCK - 1 : BLOCK, :]
    scaled = (spread(jnp.exp(after) * turned, expander) * values).astype(BF16)
    state_ref[...] = state_ref[...] * decay[BLOCK - 1 : BLOCK, :] + dot(
        inject, scaled, ((0,), (0,))
    )


def sample_kernel(
    dim,
    length_ref,
    values_ref,
    gate_ref,
    inject_ref,
    read_ref,
    step_ref,
    rate_ref,
    skip_ref,
    out_ref,
    gain_ref,
    picked_ref,
):
    samples, length, channels = values_ref.shape
    heads = channels // dim
    out_ref[...] = jnp.zeros_like(out_ref)
    gain_ref[...] = jnp.zeros_like(gain_ref)
    picked_ref[...] = jnp.zeros_like(picked_ref)
    u, s = square(length)
    own = lax.broadcasted_iota(jnp.int32, (heads, channels), 1) // dim == (
        lax.broadcasted_iota(jnp.int32, (heads, channels), 0)
    )
    at = lax.broadcasted_iota(jnp.int32, (1, length), 1)
    for k in range(samples):
        last = length_ref[k] - 1
        hot = jnp.where(lax.broadcasted_iota(jnp.int32, (PAD, length), 1) == last, 1.0, 0.0).astype(BF16)
        steps = softplus(step_ref[k])
        logs = steps * rate_ref[...]
        between = jnp.where((u > s) & (u <= last), 1.0, 0.0)
        gap = dot(logs, between, precision=EXACT)
        running = jnp.sum(jnp.where(at <= last, logs, 0.0), axis=1, keepdims=True)
        row = dot(hot, read_ref[k])
        score = dot(row.astype(BF16), inject_ref[k], ((1,), (1,)))[0:1]
        mixing = jnp.where(at <= last, score * jnp.exp(gap) * steps, 0.0).astype(BF16)
        values = values_ref[k]
        local = jnp.sum(jnp.where(own, dot(mixing, values), 0.0), axis=0, keepdims=True)
        decay = jnp.sum(jnp.where(own, jnp.exp(running), 0.0), axis=0, keepdims=True)
        value = dot(hot, values)[0:1]
        opened = silu(dot(hot, gate_ref[k])[0:1])
        out_ref[k : k + 1, :] = (local + skip_ref[...] * value) * opened
        gain_ref[k : k + 1, :] = decay * opened
        picked_ref[k : k + 1, :] = row[0:1]


def finish_rows(total, weight):
    mean = jnp.mean(total * total, axis=1, keepdims=True)
    return (total * lax.rsqrt(mean + 1e-05) * weight).astype(BF16)


def finish_kernel(
    read_ref,
    state_ref,
    out_ref,
    gain_ref,
    picked_ref,
    final_ref,
    sample_out_ref,
    sample_gain_ref,
    weight_ref,
    normed_ref,
):
    tokens = read_ref.shape[0]
    for b in range(tokens // BLOCK):
        rows = pl.ds(b * BLOCK, BLOCK)
        arrival = dot(read_ref[rows, :], state_ref[...])
        total = out_ref[rows, :].astype(F32) + arrival * gain_ref[rows, :].astype(F32)
        normed_ref[rows, :] = finish_rows(total, weight_ref[...])
    arrival = dot(picked_ref[...].astype(BF16), final_ref[...])
    total = sample_out_ref[...] + arrival * sample_gain_ref[...]
    normed_ref[pl.ds(tokens, total.shape[0]), :] = finish_rows(total, weight_ref[...])


def scan_states(state, logs, axis):
    peers, place = (lax.axis_size(axis), lax.axis_index(axis))
    before = jnp.zeros_like(state)
    total = state
    stride = 1
    while stride < peers:
        pairs = [(p, p ^ stride) for p in range(peers)]
        other = lax.ppermute(total, axis, pairs)
        other_logs = lax.ppermute(logs, axis, pairs)
        upper = (place // stride) % 2 == 1
        own_total, own_logs = total, logs
        first = jnp.where(upper, other, own_total).astype(F32)
        second = jnp.where(upper, own_total, other).astype(F32)
        second_logs = jnp.where(upper, own_logs, other_logs)
        total = (jnp.exp(second_logs) * first + second).astype(BF16)
        if stride == 1:
            before_logs = jnp.zeros_like(logs)
        before = jnp.where(
            upper,
            jnp.exp(before_logs) * other.astype(F32) + before.astype(F32),
            before.astype(F32),
        ).astype(BF16)
        before_logs = jnp.where(upper, before_logs + other_logs, before_logs)
        logs = own_logs + other_logs
        stride *= 2
    return before, total


def call(body, outs, scratch=(), flops=0, **more):
    return pl.pallas_call(
        body,
        out_shape=outs,
        scratch_shapes=list(scratch),
        compiler_params=pltpu.CompilerParams(vmem_limit_bytes=VMEM_LIMIT),
        cost_estimate=pl.CostEstimate(flops=flops, bytes_accessed=8 << 20, transcendentals=0),
        **more,
    )


def per_device(
    prompt_values,
    prompt_gate,
    prompt_inject,
    prompt_read,
    prompt_step,
    decay_log,
    skip_gain,
    norm_weight,
    out_weight,
    sample_values,
    sample_gate,
    sample_inject,
    sample_read,
    sample_step,
    sample_length,
):
    tokens, channels = prompt_values.shape
    heads = prompt_step.shape[0]
    dim = channels // heads
    entries = prompt_inject.shape[2]
    samples, length = sample_values.shape[:2]
    inject = prompt_inject.reshape(tokens, entries)
    readout = prompt_read.reshape(tokens, entries)
    rate = -jnp.exp(decay_log)[:, None]
    skip = jnp.repeat(skip_gain, dim)[None]
    weight = norm_weight[None]
    shape = jax.ShapeDtypeStruct

    state, logs = call(
        functools.partial(state_kernel, dim),
        (shape((entries, channels), BF16), shape((PAD, channels), F32)),
        [pltpu.VMEM((tokens, channels), BF16)],
        flops=2 << 30,
    )(prompt_values, inject, prompt_step, rate)

    def block(width):
        return pl.BlockSpec((BLOCK, width), lambda b: (b, 0))

    def whole(*sizes):
        return pl.BlockSpec(sizes, lambda b: (0,) * len(sizes))

    out, gain = call(
        functools.partial(local_kernel, dim),
        (shape((tokens, channels), BF16), shape((tokens, channels), BF16)),
        [
            pltpu.VMEM((entries, channels), F32),
            pltpu.VMEM((PAD, heads), F32),
            pltpu.VMEM((BLOCK, channels), F32),
        ],
        flops=8 << 30,
        grid=(tokens // BLOCK,),
        in_specs=[
            block(channels),
            block(channels),
            block(entries),
            block(entries),
            pl.BlockSpec((heads, BLOCK), lambda b: (0, b)),
            whole(heads, 1),
            whole(1, channels),
        ],
        out_specs=(block(channels), block(channels)),
    )(prompt_values, prompt_gate, inject, readout, prompt_step, rate, skip)
    padded = -(-samples // PAD) * PAD
    vmem = pl.BlockSpec(memory_space=pltpu.VMEM)
    sample_out, sample_gain, picked = call(
        functools.partial(sample_kernel, dim),
        (
            shape((padded, channels), F32),
            shape((padded, channels), F32),
            shape((padded, entries), F32),
        ),
        flops=4 << 30,
        in_specs=[pl.BlockSpec(memory_space=pltpu.SMEM)] + [vmem] * 7,
    )(
        sample_length,
        sample_values,
        sample_gate,
        sample_inject.reshape(samples, length, entries),
        sample_read.reshape(samples, length, entries),
        sample_step.transpose(1, 0, 2),
        rate,
        skip,
    )
    before, final = scan_states(state, logs[:1], "ctx")
    normed = call(finish_kernel, shape((tokens + padded, channels), BF16), flops=1 << 30)(
        readout, before, out, gain, picked, final, sample_out, sample_gain, weight
    )
    return project(normed, out_weight, tokens, samples)


def project(normed, out_weight, tokens, samples):
    share = dot(normed, out_weight).astype(BF16)
    mixed = lax.psum_scatter(share, "head", scatter_dimension=1, tiled=True)
    return mixed[:tokens].T, mixed[tokens : tokens + samples].T


def solution(mesh):
    in_specs = (
        P("ctx", "head"),
        P("ctx", "head"),
        P("ctx", "head", None),
        P("ctx", "head", None),
        P("head", "ctx"),
        P("head"),
        P("head"),
        P("head"),
        P("head", None),
        P("ctx", None, "head"),
        P("ctx", None, "head"),
        P("ctx", None, "head", None),
        P("ctx", None, "head", None),
        P("head", "ctx", None),
        P("ctx"),
    )
    out_specs = (P("head", "ctx"), P("head", "ctx"))
    return jax.shard_map(
        per_device, mesh=mesh, in_specs=in_specs, out_specs=out_specs, check_vma=False
    )
```

```python
import functools

import jax
import jax.numpy as jnp
from jax import lax
from jax.experimental import pallas as pl
from jax.experimental.pallas import tpu as pltpu
from jax.sharding import PartitionSpec as P

BLOCK = 128
LANES = 128
PAD = 8
F32 = jnp.float32
BF16 = jnp.bfloat16
EXACT = lax.Precision.HIGHEST
VMEM_LIMIT = 60 * 1024 * 1024


def dot(a, b, dims=((1,), (0,)), precision=None):
    return lax.dot_general(a, b, (dims, ((), ())), precision=precision, preferred_element_type=F32)


def softplus(v):
    return jnp.maximum(v, 0.0) + jnp.log1p(jnp.exp(-jnp.abs(v)))


def silu(v):
    return v / (1.0 + jnp.exp(-v))


def spread(w, expander):
    high = w.astype(BF16)
    low = (w - high.astype(F32)).astype(BF16)
    return dot(jnp.concatenate([high, low], axis=1), expander)


def expander_of(heads, dim):
    row = lax.broadcasted_iota(jnp.int32, (2 * heads, heads * dim), 0)
    lane = lax.broadcasted_iota(jnp.int32, (2 * heads, heads * dim), 1)
    head = lane // dim
    return jnp.where((row == head) | (row == head + heads), 1.0, 0.0).astype(BF16)


def square(n):
    return (
        lax.broadcasted_iota(jnp.int32, (n, n), 0),
        lax.broadcasted_iota(jnp.int32, (n, n), 1),
    )


def state_kernel(dim, values_ref, inject_ref, step_ref, rate_ref, state_ref, log_ref, scaled_ref):
    tokens, channels = values_ref.shape
    heads = channels // dim
    steps = softplus(step_ref[...])
    logs = steps * rate_ref[...]
    i, j = square(tokens)
    after = dot(jnp.where(j > i, 1.0, 0.0), logs, ((1,), (1,)), EXACT)
    total = dot(jnp.ones((PAD, tokens), F32), logs, ((1,), (1,)), EXACT)
    turned = dot(jnp.where(i == j, 1.0, 0.0), steps, ((1,), (1,)), EXACT)
    weight = jnp.exp(after) * turned
    expander = expander_of(heads, dim)
    for b in range(tokens // BLOCK):
        rows = pl.ds(b * BLOCK, BLOCK)
        wide = spread(weight[b * BLOCK : (b + 1) * BLOCK], expander)
        scaled_ref[rows, :] = (wide * values_ref[rows, :].astype(F32)).astype(BF16)
    state_ref[...] = dot(inject_ref[...], scaled_ref[...], ((0,), (0,))).astype(BF16)
    log_ref[...] = dot(total, expander[:heads].astype(F32), precision=EXACT)


def local_kernel(
    dim,
    values_ref,
    gate_ref,
    inject_ref,
    read_ref,
    step_ref,
    rate_ref,
    skip_ref,
    out_ref,
    gain_ref,
    state_ref,
    offset_ref,
    part_ref,
):
    channels = values_ref.shape[1]
    heads = channels // dim

    @pl.when(pl.program_id(0) == 0)
    def _():
        state_ref[...] = jnp.zeros_like(state_ref)
        offset_ref[...] = jnp.zeros_like(offset_ref)

    steps = softplus(step_ref[...])
    logs = steps * rate_ref[...]
    i, j = square(BLOCK)
    lower = jnp.where(i >= j, 1.0, 0.0)
    running = dot(logs, lower, ((1,), (1,)), EXACT)
    running_t = dot(lower, logs, ((1,), (1,)), EXACT)
    after = dot(jnp.where(j > i, 1.0, 0.0), logs, ((1,), (1,)), EXACT)
    turned = dot(jnp.where(i == j, 1.0, 0.0), steps, ((1,), (1,)), EXACT)
    expander = expander_of(heads, dim)
    inject = inject_ref[...]
    readout = read_ref[...]
    scores = jnp.where(i >= j, dot(readout, inject, ((1,), (1,))), 0.0)
    per = LANES // dim
    lane = lax.broadcasted_iota(jnp.int32, (BLOCK, LANES), 1)
    for k in range(heads // per):
        cols = slice(k * LANES, (k + 1) * LANES)
        pair = values_ref[:, cols]
        mixes, parts = [], []
        for q in range(per):
            h = k * per + q
            gap = jnp.minimum(running_t[:, h : h + 1] - running[h : h + 1, :], 0.0)
            mixes.append((scores * jnp.exp(gap) * steps[h : h + 1, :]).astype(BF16))
            parts.append(jnp.where(lane // dim == q, pair, jnp.zeros_like(pair)))
        part_ref[:, cols] = dot(jnp.concatenate(mixes, axis=1), jnp.concatenate(parts, axis=0))
    decay = spread(jnp.exp(running_t), expander)
    values = values_ref[...].astype(F32)
    opened = silu(gate_ref[...].astype(F32))
    total = part_ref[...] + skip_ref[...] * values
    total = total + dot(readout, state_ref[...].astype(BF16)) * decay
    out_ref[...] = (total * opened).astype(BF16)
    offset = offset_ref[0:1, :]
    gain_ref[...] = (opened * spread(jnp.exp(running_t + offset), expander)).astype(BF16)
    offset_ref[0:1, :] = offset + running_t[BLOCK - 1 : BLOCK, :]
    scaled = (spread(jnp.exp(after) * turned, expander) * values).astype(BF16)
    state_ref[...] = state_ref[...] * decay[BLOCK - 1 : BLOCK, :] + dot(
        inject, scaled, ((0,), (0,))
    )


def sample_kernel(
    dim,
    length_ref,
    values_ref,
    gate_ref,
    inject_ref,
    read_ref,
    step_ref,
    rate_ref,
    skip_ref,
    out_ref,
    gain_ref,
    picked_ref,
):
    samples, length, channels = values_ref.shape
    heads = channels // dim
    out_ref[...] = jnp.zeros_like(out_ref)
    gain_ref[...] = jnp.zeros_like(gain_ref)
    picked_ref[...] = jnp.zeros_like(picked_ref)
    u, s = square(length)
    own = lax.broadcasted_iota(jnp.int32, (heads, channels), 1) // dim == (
        lax.broadcasted_iota(jnp.int32, (heads, channels), 0)
    )
    at = lax.broadcasted_iota(jnp.int32, (1, length), 1)
    for k in range(samples):
        last = length_ref[k] - 1
        hot = jnp.where(lax.broadcasted_iota(jnp.int32, (PAD, length), 1) == last, 1.0, 0.0).astype(BF16)
        steps = softplus(step_ref[k])
        logs = steps * rate_ref[...]
        between = jnp.where((u > s) & (u <= last), 1.0, 0.0)
        gap = dot(logs, between, precision=EXACT)
        running = jnp.sum(jnp.where(at <= last, logs, 0.0), axis=1, keepdims=True)
        row = dot(hot, read_ref[k])
        score = dot(row.astype(BF16), inject_ref[k], ((1,), (1,)))[0:1]
        mixing = jnp.where(at <= last, score * jnp.exp(gap) * steps, 0.0).astype(BF16)
        values = values_ref[k]
        local = jnp.sum(jnp.where(own, dot(mixing, values), 0.0), axis=0, keepdims=True)
        decay = jnp.sum(jnp.where(own, jnp.exp(running), 0.0), axis=0, keepdims=True)
        value = dot(hot, values)[0:1]
        opened = silu(dot(hot, gate_ref[k])[0:1])
        out_ref[k : k + 1, :] = (local + skip_ref[...] * value) * opened
        gain_ref[k : k + 1, :] = decay * opened
        picked_ref[k : k + 1, :] = row[0:1]


def finish_rows(total, weight):
    mean = jnp.mean(total * total, axis=1, keepdims=True)
    return (total * lax.rsqrt(mean + 1e-05) * weight).astype(BF16)


def finish_kernel(
    read_ref,
    state_ref,
    out_ref,
    gain_ref,
    picked_ref,
    final_ref,
    sample_out_ref,
    sample_gain_ref,
    weight_ref,
    normed_ref,
):
    tokens = read_ref.shape[0]
    for b in range(tokens // BLOCK):
        rows = pl.ds(b * BLOCK, BLOCK)
        arrival = dot(read_ref[rows, :], state_ref[...])
        total = out_ref[rows, :].astype(F32) + arrival * gain_ref[rows, :].astype(F32)
        normed_ref[rows, :] = finish_rows(total, weight_ref[...])
    arrival = dot(picked_ref[...].astype(BF16), final_ref[...])
    total = sample_out_ref[...] + arrival * sample_gain_ref[...]
    normed_ref[pl.ds(tokens, total.shape[0]), :] = finish_rows(total, weight_ref[...])


def scan_states(state, logs, axis):
    peers, place = (lax.axis_size(axis), lax.axis_index(axis))

    def swap(value, stride):
        return lax.ppermute(value, axis, [(p, p ^ stride) for p in range(peers)])

    def join(first, second, second_logs):
        return jnp.exp(second_logs) * first.astype(F32) + second.astype(F32)

    odd = place % 2 == 1
    other, other_logs = swap(state, 1), swap(logs, 1)
    half = state.shape[0] // 2

    def own_half(value):
        return lax.dynamic_slice_in_dim(value, (place % 2) * half, half, 0)

    mine, theirs = own_half(state), own_half(other)
    total = join(
        jnp.where(odd, theirs, mine), jnp.where(odd, mine, theirs), jnp.where(odd, logs, other_logs)
    ).astype(BF16)
    total_logs = logs + other_logs
    before, before_logs = jnp.zeros(total.shape, F32), jnp.zeros_like(logs)
    stride = 2
    while stride < peers:
        upper = (place // stride) % 2 == 1
        far, far_logs = swap(total, stride), swap(total_logs, stride)
        before = jnp.where(upper, join(far, before, before_logs), before)
        before_logs = jnp.where(upper, before_logs + far_logs, before_logs)
        total = join(
            jnp.where(upper, far, total),
            jnp.where(upper, total, far),
            jnp.where(upper, total_logs, far_logs),
        ).astype(BF16)
        total_logs = total_logs + far_logs
        stride *= 2
    pack = jnp.stack([before.astype(BF16), total])
    swapped = swap(pack, 1)
    low, high = jnp.where(odd, swapped, pack), jnp.where(odd, pack, swapped)
    both = jnp.concatenate([low, high], axis=1)
    entered = jnp.where(odd, join(both[0], other, other_logs), both[0].astype(F32))
    return entered.astype(BF16), both[1]


def call(body, outs, scratch=(), flops=0, **more):
    return pl.pallas_call(
        body,
        out_shape=outs,
        scratch_shapes=list(scratch),
        compiler_params=pltpu.CompilerParams(vmem_limit_bytes=VMEM_LIMIT),
        cost_estimate=pl.CostEstimate(flops=flops, bytes_accessed=8 << 20, transcendentals=0),
        **more,
    )


def per_device(
    prompt_values,
    prompt_gate,
    prompt_inject,
    prompt_read,
    prompt_step,
    decay_log,
    skip_gain,
    norm_weight,
    out_weight,
    sample_values,
    sample_gate,
    sample_inject,
    sample_read,
    sample_step,
    sample_length,
):
    tokens, channels = prompt_values.shape
    heads = prompt_step.shape[0]
    dim = channels // heads
    entries = prompt_inject.shape[2]
    samples, length = sample_values.shape[:2]
    inject = prompt_inject.reshape(tokens, entries)
    readout = prompt_read.reshape(tokens, entries)
    rate = -jnp.exp(decay_log)[:, None]
    skip = jnp.repeat(skip_gain, dim)[None]
    weight = norm_weight[None]
    shape = jax.ShapeDtypeStruct

    state, logs = call(
        functools.partial(state_kernel, dim),
        (shape((entries, channels), BF16), shape((PAD, channels), F32)),
        [pltpu.VMEM((tokens, channels), BF16)],
        flops=2 << 30,
    )(prompt_values, inject, prompt_step, rate)

    def block(width):
        return pl.BlockSpec((BLOCK, width), lambda b: (b, 0))

    def whole(*sizes):
        return pl.BlockSpec(sizes, lambda b: (0,) * len(sizes))

    out, gain = call(
        functools.partial(local_kernel, dim),
        (shape((tokens, channels), BF16), shape((tokens, channels), BF16)),
        [
            pltpu.VMEM((entries, channels), F32),
            pltpu.VMEM((PAD, heads), F32),
            pltpu.VMEM((BLOCK, channels), F32),
        ],
        flops=8 << 30,
        grid=(tokens // BLOCK,),
        in_specs=[
            block(channels),
            block(channels),
            block(entries),
            block(entries),
            pl.BlockSpec((heads, BLOCK), lambda b: (0, b)),
            whole(heads, 1),
            whole(1, channels),
        ],
        out_specs=(block(channels), block(channels)),
    )(prompt_values, prompt_gate, inject, readout, prompt_step, rate, skip)
    padded = -(-samples // (2 * PAD)) * 2 * PAD
    vmem = pl.BlockSpec(memory_space=pltpu.VMEM)
    sample_out, sample_gain, picked = call(
        functools.partial(sample_kernel, dim),
        (
            shape((padded, channels), F32),
            shape((padded, channels), F32),
            shape((padded, entries), F32),
        ),
        flops=4 << 30,
        in_specs=[pl.BlockSpec(memory_space=pltpu.SMEM)] + [vmem] * 7,
    )(
        sample_length,
        sample_values,
        sample_gate,
        sample_inject.reshape(samples, length, entries),
        sample_read.reshape(samples, length, entries),
        sample_step.transpose(1, 0, 2),
        rate,
        skip,
    )
    before, final = scan_states(state, logs[:1], "ctx")
    normed = call(finish_kernel, shape((tokens + padded, channels), BF16), flops=1 << 30)(
        readout, before, out, gain, picked, final, sample_out, sample_gain, weight
    )
    return project(normed, out_weight, tokens, samples)


def project_kernel(
    n,
    normed_ref,
    weight_ref,
    out_ref,
    tiles,
    sent,
    from_low,
    from_high,
    tile_sems,
    sent_sems,
    low_sems,
    high_sems,
):
    place = lax.axis_index("head")
    chunks, _, width = out_ref.shape

    def tile_copy(d, c):
        start = (d * chunks + c) * width
        if not isinstance(start, int):
            start = pl.multiple_of(start, width)
        return pltpu.make_async_copy(
            weight_ref.at[:, pl.ds(start, width)],
            tiles.at[d, c],
            tile_sems.at[d, c],
        )

    for k in range((n + 1) // 2):
        for c in range(chunks):
            for d in sorted({n - 1 - k, k}, reverse=True):
                tile_copy(d, c).start()

    barrier = pltpu.get_barrier_semaphore()

    def greet(to):
        pl.semaphore_signal(
            barrier, inc=1, device_id={"head": to}, device_id_type=pl.DeviceIdType.MESH
        )

    @pl.when(place > 0)
    def _():
        greet(place - 1)

    @pl.when(place < n - 1)
    def _():
        greet(place + 1)

    inside = (place > 0) & (place < n - 1)

    @pl.when(inside)
    def _():
        pl.semaphore_wait(barrier, 2)

    @pl.when(jnp.logical_not(inside))
    def _():
        pl.semaphore_wait(barrier, 1)

    def hop(d, c, landing, sems, to):
        return pltpu.make_async_remote_copy(
            src_ref=sent.at[d, c],
            dst_ref=landing.at[d, c],
            send_sem=sent_sems.at[d, c],
            recv_sem=sems.at[d, c],
            device_id={"head": to},
            device_id_type=pl.DeviceIdType.MESH,
        )

    def up(d, c):
        return hop(d, c, from_low, low_sems, place + 1)

    def down(d, c):
        return hop(d, c, from_high, high_sems, place - 1)

    def share(d, c):
        tile_copy(d, c).wait()
        return dot(normed_ref[...], tiles[d, c])

    def pass_on(d, c, move, landing, fed):
        sent[d, c] = share(d, c).astype(BF16)

        @pl.when(fed)
        def _():
            move(d, c).wait_recv()
            sent[d, c] = (sent[d, c].astype(F32) + landing[d, c].astype(F32)).astype(BF16)

        move(d, c).start()

    def turn(t, carry):
        k, c = t // chunks, t % chunks

        @pl.when(place < n - 1 - k)
        def _():
            pass_on(n - 1 - k, c, up, from_low, place > 0)

        @pl.when(place > k)
        def _():
            pass_on(k, c, down, from_high, place < n - 1)

        return carry

    lax.fori_loop(0, (n - 1) * chunks, turn, 0)

    def own(c, carry):
        out_ref[c] = share(place, c).astype(BF16)
        return carry

    lax.fori_loop(0, chunks, own, 0)

    def gather(c, carry):
        @pl.when(place < n - 1)
        def _():
            down(place, c).wait_recv()
            out_ref[c] = (out_ref[c].astype(F32) + from_high[place, c].astype(F32)).astype(BF16)

        @pl.when(place > 0)
        def _():
            up(place, c).wait_recv()
            out_ref[c] = (out_ref[c].astype(F32) + from_low[place, c].astype(F32)).astype(BF16)

        return carry

    lax.fori_loop(0, chunks, gather, 0)

    def drain(t, carry):
        d, c = t // chunks, t % chunks

        @pl.when(d > place)
        def _():
            up(d, c).wait_send()

        @pl.when(d < place)
        def _():
            down(d, c).wait_send()

        return carry

    lax.fori_loop(0, n * chunks, drain, 0)


def project(normed, out_weight, tokens, samples):
    n = lax.axis_size("head")
    rows, depth = normed.shape
    width = 2 * LANES
    chunks = out_weight.shape[1] // n // width
    slots = pltpu.VMEM((n, chunks, rows, width), BF16)
    sems = pltpu.SemaphoreType.DMA((n, chunks))
    mixed = pl.pallas_call(
        functools.partial(project_kernel, n),
        out_shape=jax.ShapeDtypeStruct((chunks, rows, width), BF16),
        in_specs=[
            pl.BlockSpec(memory_space=pltpu.VMEM),
            pl.BlockSpec(memory_space=pl.ANY),
        ],
        out_specs=pl.BlockSpec(memory_space=pltpu.VMEM),
        scratch_shapes=[
            pltpu.VMEM((n, chunks, depth, width), BF16),
            slots,
            slots,
            slots,
            sems,
            sems,
            sems,
            sems,
        ],
        compiler_params=pltpu.CompilerParams(
            collective_id=0, has_side_effects=True, vmem_limit_bytes=VMEM_LIMIT
        ),
    )(normed, out_weight)
    mixed = mixed.transpose(0, 2, 1).reshape(chunks * width, rows)
    return mixed[:, :tokens], mixed[:, tokens : tokens + samples]


def solution(mesh):
    in_specs = (
        P("ctx", "head"),
        P("ctx", "head"),
        P("ctx", "head", None),
        P("ctx", "head", None),
        P("head", "ctx"),
        P("head"),
        P("head"),
        P("head"),
        P("head", None),
        P("ctx", None, "head"),
        P("ctx", None, "head"),
        P("ctx", None, "head", None),
        P("ctx", None, "head", None),
        P("head", "ctx", None),
        P("ctx"),
    )
    out_specs = (P("head", "ctx"), P("head", "ctx"))
    return jax.shard_map(
        per_device, mesh=mesh, in_specs=in_specs, out_specs=out_specs, check_vma=False
    )
```
